32 devices in a mesh: tile: 8 (over z, x), slab: 4 (over y, core).
Axes of the slice: x: 2, y: 2, z: 4, core: 2. Of those that a mesh axis runs over, the one named last changes fastest.
Arguments:
- object_field: bfloat16 [2, 8, 1024, 512], P(None, 'slab', 'tile')
- probe_wave: bfloat16 [2, 128, 128], replicated, may hold values from -6 to 6
- prop_phase: float32 [128, 128], replicated, may hold values from -3.140625 to 3.140625
- intensity: float32 [16, 128, 128], P('tile'), may hold values from 0 to 4
- patch_rows: int32 [16], replicated, may hold values from 0 to 127
- patch_cols: int32 [16], replicated, may hold values from 0 to 384
Outputs:
- grad_object: bfloat16 [2, 8, 1024, 512], P(None, 'slab', 'tile')
The draws below stay inside these ranges and needn't reach their ends.
Inputs may be any that keep to these rules, and one draw needn't show every extreme that they name: `patch_rows`: a window of tile t covers rows of tile t and of the next tile (the first tile after the last).
All inputs are finite; a program needn't handle non-finite values.
Results may differ from the reference program's by a relative error of at most 0.005.
Values may be sent and summed in bfloat16 or wider, within the bound.
A program may use at most 64 MiB of HBM per device.

```python
import math
import jax
import jax.numpy as jnp
from jax import lax

WIN = 128
OCOL = 512
POS_DEV = 2
SLICES = 8
ROWS = 1024
POS = 16
N_TILE = 8


def draw_object_field(key, part):
    amp_key, phase_key = jax.random.split(jax.random.fold_in(key, 11))
    field_shape = (SLICES, ROWS, OCOL)
    magnitude = 0.9 + 0.2 * jax.random.uniform(amp_key, field_shape, jnp.float32)
    phases = jax.random.uniform(phase_key, field_shape, jnp.float32, -math.pi, math.pi)
    return jnp.stack([magnitude * jnp.cos(phases), magnitude * jnp.sin(phases)]).astype(jnp.bfloat16)


def touch_ends(result, rng, least, top_value):
    shape = result.shape
    index_at = [jax.random.randint(jax.random.fold_in(rng, axis), (), 0, shape[axis]) for axis in range(len(shape))]
    result = result.at[tuple(index_at)].set(least)
    longest = shape.index(max(shape))
    index_at[longest] = (index_at[longest] + 1) % shape[longest]
    return result.at[tuple(index_at)].set(top_value)


def levels(rng, extent, pieces, low, largest):
    def one(dim, parts):
        draws = jax.random.uniform(jax.random.fold_in(jax.random.fold_in(rng, 6), dim), (parts,), jnp.float32, low / len(pieces), largest / len(pieces))
        return jnp.repeat(jnp.exp(draws), extent[dim] // parts).reshape((-1,) + (1,) * (len(extent) - dim - 1))

    level = one(*pieces[0])
    for cut in pieces[1:]:
        level = level * one(*cut)
    return level


def bell_draw(own_key, dims, width, bound, kind=jnp.bfloat16):
    return jnp.clip(width * jax.random.normal(own_key, dims, jnp.float32), -bound, bound).astype(kind)


def setup_inputs(seed: int = 0) -> dict:
    key_list = jax.random.split(jax.random.key(seed), 7)
    return {
        "object_field": draw_object_field(jax.random.fold_in(key_list[6], 71), 0),
        "probe_wave": bell_draw(key_list[1], (2, WIN, WIN), 1.0, 6.0),
        "prop_phase": jnp.clip(jax.random.uniform(key_list[2], (WIN, WIN), jnp.float32, -3.140625, 3.140625), -3.140625, 3.140625),
        "intensity": jnp.clip(4.0 * jax.random.uniform(key_list[3], (POS, WIN, WIN), jnp.float32) ** levels(key_list[3], (POS, WIN, WIN), ((0, 8),), -0.2, 0.2), 0.0, 4.0),
        "patch_rows": touch_ends(jax.random.randint(key_list[4], (POS,), 0, WIN), jax.random.fold_in(key_list[4], 1), 0, WIN - 1).astype(jnp.int32),
        "patch_cols": touch_ends(jax.random.randint(key_list[5], (POS,), 0, OCOL - WIN + 1), jax.random.fold_in(key_list[5], 1), 0, OCOL - WIN).astype(jnp.int32),
    }


def fourier_tables(window, exponent_sign):
    indices = jnp.arange(window, dtype=jnp.int32)
    product = indices[:, None] * indices[None, :] % window
    angles = product.astype(jnp.float32) * (exponent_sign * 2.0 * math.pi / window)
    scaling = 1.0 / math.sqrt(window)
    real_part = jnp.cos(angles) * scaling
    imag_part = jnp.sin(angles) * scaling
    left_table = jnp.concatenate([real_part, imag_part], axis=0)
    right_table = jnp.concatenate([jnp.concatenate([real_part, imag_part], axis=1), jnp.concatenate([-imag_part, real_part], axis=1)], axis=0)
    return (left_table, right_table)

def transform(field_in, tables, window):
    left_table, right_table = tables
    first_pass = jnp.dot(field_in, right_table, precision=lax.Precision.HIGHEST, preferred_element_type=jnp.float32)
    second_pass = jnp.dot(left_table, first_pass, precision=lax.Precision.HIGHEST, preferred_element_type=jnp.float32)
    upper_half = second_pass[:window]
    lower_half = second_pass[window:]
    return jnp.concatenate([upper_half[:, :window] - lower_half[:, window:], upper_half[:, window:] + lower_half[:, :window]], axis=1)

def complex_times(left_side, right_side, window):
    left_re = left_side[..., :window].astype(jnp.float32)
    left_im = left_side[..., window:].astype(jnp.float32)
    right_re = right_side[..., :window].astype(jnp.float32)
    right_im = right_side[..., window:].astype(jnp.float32)
    return jnp.concatenate([left_re * right_re - left_im * right_im, left_re * right_im + left_im * right_re], axis=-1)

def conj_times(left_side, right_side, window):
    left_re = left_side[..., :window].astype(jnp.float32)
    left_im = left_side[..., window:].astype(jnp.float32)
    right_re = right_side[..., :window].astype(jnp.float32)
    right_im = right_side[..., window:].astype(jnp.float32)
    return jnp.concatenate([left_re * right_re + left_im * right_im, left_re * right_im - left_im * right_re], axis=-1)

def add_block(gradient, block, column, window, layers):
    zero_index = jnp.zeros((), jnp.int32)
    paired = jnp.stack([block[..., :window], block[..., window:]])
    where_at = (zero_index, zero_index, zero_index, column.astype(jnp.int32))
    current = lax.dynamic_slice(gradient, where_at, (2, layers, window, window))
    return lax.dynamic_update_slice(gradient, current + paired, where_at)

def place_rows(term_block, row_start, window, layers):
    zero_index = jnp.zeros((), jnp.int32)
    placed = jnp.zeros((layers, 2 * window, 2 * window), jnp.float32)
    return lax.dynamic_update_slice(placed, term_block, (zero_index, row_start.astype(jnp.int32), zero_index))

def reference(object_field, probe_wave, prop_phase, intensity, patch_rows, patch_cols):
    window = WIN
    forward_tables = fourier_tables(window, -1.0)
    backward_tables = fourier_tables(window, 1.0)
    propagator = jnp.concatenate([jnp.cos(prop_phase), jnp.sin(prop_phase)], axis=1)
    incoming_start = jnp.concatenate([probe_wave[0], probe_wave[1]], axis=1).astype(jnp.float32)
    offsets = jnp.arange(window, dtype=jnp.int32)

    def one_position(position):
        tile_index = position // POS_DEV
        row_index = (tile_index * window + patch_rows[position] + offsets) % ROWS
        picked = jnp.take(object_field, row_index, axis=2)
        cut_window = lax.dynamic_slice_in_dim(picked, patch_cols[position].astype(jnp.int32), window, axis=3)
        patches = jnp.concatenate([cut_window[0], cut_window[1]], axis=2)
        incoming = incoming_start
        stored = []
        outgoing = incoming
        for layer_index in range(SLICES):
            stored.append(incoming)
            outgoing = complex_times(incoming, patches[layer_index], window)
            if layer_index < SLICES - 1:
                moved = complex_times(propagator, transform(outgoing, forward_tables, window), window)
                incoming = transform(moved, backward_tables, window)
        far_field = transform(outgoing, forward_tables, window)
        far_power = far_field[:, :window] ** 2 + far_field[:, window:] ** 2
        misfit = far_power - intensity[position]
        far_grad = jnp.concatenate([misfit, misfit], axis=1) * far_field
        out_grad = transform(far_grad, backward_tables, window)
        patch_terms = [None] * SLICES
        for layer_index in reversed(range(SLICES)):
            patch_terms[layer_index] = conj_times(stored[layer_index], out_grad, window)
            if layer_index > 0:
                in_grad = conj_times(patches[layer_index], out_grad, window)
                returned = conj_times(propagator, transform(in_grad, forward_tables, window), window)
                out_grad = transform(returned, backward_tables, window)
        return jnp.stack(patch_terms)
    grad_terms = lax.map(one_position, jnp.arange(POS, dtype=jnp.int32))

    def one_tile(tile_index):
        gradient = jnp.zeros((2, SLICES, window, OCOL), jnp.float32)
        tile_before = (tile_index + N_TILE - 1) % N_TILE
        for member in range(POS_DEV):
            own_position = tile_index * POS_DEV + member
            placed = place_rows(grad_terms[own_position], patch_rows[own_position], window, SLICES)
            gradient = add_block(gradient, placed[:, :window], patch_cols[own_position], window, SLICES)
            prior_position = tile_before * POS_DEV + member
            prior_placed = place_rows(grad_terms[prior_position], patch_rows[prior_position], window, SLICES)
            gradient = add_block(gradient, prior_placed[:, window:], patch_cols[prior_position], window, SLICES)
        return gradient.astype(jnp.bfloat16)
    tiled = lax.map(one_tile, jnp.arange(N_TILE, dtype=jnp.int32))
    return jnp.moveaxis(tiled, 0, 2).reshape(2, SLICES, ROWS, OCOL)
```

```python
import functools
import math

import jax
import jax.numpy as jnp
import numpy as np
from jax import lax
from jax.experimental import pallas as pl
from jax.experimental.pallas import tpu as pltpu
from jax.sharding import PartitionSpec as P

F32 = jnp.float32
BF16 = jnp.bfloat16


def fourier_parts(window):
    index = np.arange(window)
    angle = (index[:, None] * index[None, :] % window) * (-2.0 * math.pi / window)
    real = np.cos(angle) / math.sqrt(window)
    imag = np.sin(angle) / math.sqrt(window)
    big = np.block([[real, imag], [-imag, real]]).astype(np.float32)
    high = big.astype(BF16)
    low = (big - high.astype(np.float32)).astype(BF16)
    right = np.concatenate([high, high, low], axis=0)
    left = np.concatenate([high.T, high.T, low.T], axis=1)
    return right, left


def split(value):
    high = value.astype(BF16)
    return high, (value - high.astype(F32)).astype(BF16)


def transform(field, right, left, window):
    count = len(field)
    high, low = split(
        jnp.concatenate([jnp.concatenate([re, im], axis=1) for re, im in field], axis=0)
    )
    first = jnp.dot(
        jnp.concatenate([high, low, high], axis=1), right[...], preferred_element_type=F32
    )
    rows = [first[p * window : (p + 1) * window] for p in range(count)]
    high, low = split(
        jnp.concatenate(
            [jnp.concatenate([r[:, :window], r[:, window:]], axis=0) for r in rows], axis=1
        )
    )
    second = jnp.dot(
        left[...], jnp.concatenate([high, low, high], axis=0), preferred_element_type=F32
    )
    out = []
    for p in range(count):
        block = second[:, p * window : (p + 1) * window]
        out.append((block[:window], block[window:]))
    return out


def times(a, b):
    return a[0] * b[0] - a[1] * b[1], a[0] * b[1] + a[1] * b[0]


def conj_times(a, b):
    return a[0] * b[0] + a[1] * b[1], a[0] * b[1] - a[1] * b[0]


def conj(a):
    return a[0], -a[1]


def load(ref, lead, count, window):
    out = []
    for p in range(count):
        block = ref[lead, p].astype(F32)
        out.append((block[:, :window], block[:, window:]))
    return out


def store(ref, lead, field):
    for p, (re, im) in enumerate(field):
        ref[lead, p] = jnp.concatenate([re, im], axis=1).astype(ref.dtype)


def chain(patches, probe, phase, measured, right, left, psi, work, terms, layers):
    slices, count, window = patches.shape[0], patches.shape[1], probe.shape[1]
    first_own = lax.axis_index("slab") * layers
    prop = (jnp.cos(phase[...]), jnp.sin(phase[...]))
    prop_store = work.at[count]
    prop_store[...] = jnp.concatenate(prop, axis=1)

    def propagator():
        value = prop_store[...]
        return value[:, :window], value[:, window:]

    run = functools.partial(transform, right=right, left=left, window=window)
    start = (probe[0].astype(F32), probe[1].astype(F32))
    store(psi, 0, [start] * count)

    def forward(j, carried):
        chi = [
            times(a, b)
            for a, b in zip(load(psi, j, count, window), load(patches, j, count, window))
        ]
        moved = run(chi)
        prop = propagator()
        back = run([conj(times(prop, f)) for f in moved])
        store(psi, j + 1, [conj(f) for f in back])
        return carried

    lax.fori_loop(0, slices - 1, forward, 0)
    last = slices - 1
    chi = [
        times(a, b)
        for a, b in zip(load(psi, last, count, window), load(patches, last, count, window))
    ]
    far = run(chi)
    shaped = []
    for p, (re, im) in enumerate(far):
        misfit = re * re + im * im - measured[p]
        shaped.append((misfit * re, -(misfit * im)))
    grad = [conj(f) for f in run(shaped)]
    for p in range(count):
        work[p] = jnp.concatenate(grad[p], axis=1)

    def own_term(j):
        @pl.when((j >= first_own) & (j < first_own + layers))
        def _():
            for p in range(count):
                block = work[p]
                wave = psi[j, p]
                term = conj_times(
                    (wave[:, :window], wave[:, window:]), (block[:, :window], block[:, window:])
                )
                terms[j - first_own, p] = jnp.concatenate(term, axis=1)

    def backward(i, carried):
        j = last - i
        own_term(j)
        grads = []
        for p in range(count):
            block = work[p]
            grads.append((block[:, :window], block[:, window:]))
        inner = [conj_times(a, b) for a, b in zip(load(patches, j, count, window), grads)]
        moved = run(inner)
        prop = propagator()
        back = run([conj(conj_times(prop, f)) for f in moved])
        for p in range(count):
            work[p] = jnp.concatenate(conj(back[p]), axis=1)
        return carried

    lax.fori_loop(0, last, backward, 0)
    own_term(0)


def chain_kernel(patches, probe, phase, measured, right, left, terms, psi, work):
    chain(patches, probe, phase, measured, right, left, psi, work, terms, terms.shape[0])


def body(object_field, probe_wave, prop_phase, intensity, patch_rows, patch_cols):
    window = probe_wave.shape[1]
    layers = object_field.shape[1]
    columns = object_field.shape[3]
    count = intensity.shape[0]
    tiles = lax.axis_size("tile")
    sections = lax.axis_size("slab")
    slices = sections * layers
    here = lax.axis_index("tile")
    before = (here + tiles - 1) % tiles
    own_rows = lax.dynamic_slice_in_dim(patch_rows, here * count, count)
    own_cols = lax.dynamic_slice_in_dim(patch_cols, here * count, count)
    prior_cols = lax.dynamic_slice_in_dim(patch_cols, before * count, count)
    right, left = fourier_parts(window)

    def column_pick(cols):
        at = cols[:, None] + jnp.arange(window, dtype=jnp.int32)[None, :]
        return jnp.arange(columns, dtype=jnp.int32)[:, None, None] == at[None]

    def cut(cols):
        return jnp.einsum(
            "zlrc,cpk->lprzk", object_field, column_pick(cols).astype(BF16)
        ).reshape(layers, count, window, 2 * window)

    def shift(value, by):
        peers = lax.axis_size("tile")
        return lax.ppermute(value, "tile", [(i, (i + by) % peers) for i in range(peers)])

    arrived = shift(cut(prior_cols), -1)
    stacked = jnp.concatenate([cut(own_cols), arrived], axis=2)
    row_at = own_rows[:, None] + jnp.arange(window, dtype=jnp.int32)[None, :]
    row_pick = jnp.arange(2 * window, dtype=jnp.int32)[None, None, :] == row_at[:, :, None]
    mine = jnp.einsum("pir,lprk->lpik", row_pick.astype(BF16), stacked)
    patches = lax.all_gather(mine, "slab", axis=0, tiled=True)
    terms = pl.pallas_call(
        chain_kernel,
        out_shape=jax.ShapeDtypeStruct((layers, count, window, 2 * window), F32),
        in_specs=[pl.BlockSpec(memory_space=pltpu.VMEM)] * 6,
        out_specs=pl.BlockSpec(memory_space=pltpu.VMEM),
        scratch_shapes=[
            pltpu.VMEM((slices, count, window, 2 * window), F32),
            pltpu.VMEM((count + 1, window, 2 * window), F32),
        ],
        compiler_params=pltpu.CompilerParams(vmem_limit_bytes=60 * 1024 * 1024),
    )(patches, probe_wave, prop_phase, intensity, jnp.asarray(right), jnp.asarray(left))
    placed = jnp.einsum(
        "pir,lpik->lprk", row_pick.astype(F32), terms, precision=lax.Precision.HIGH
    )
    received = shift(placed[:, :, window:].astype(BF16), 1)
    pieces = jnp.concatenate([placed[:, :, :window], received.astype(F32)], axis=1)
    picks = jnp.concatenate([column_pick(own_cols), column_pick(prior_cols)], axis=1)
    gradient = jnp.einsum(
        "lprzk,cpk->zlrc",
        pieces.reshape(layers, 2 * count, window, 2, window),
        picks.astype(F32),
        precision=lax.Precision.HIGH,
    )
    return gradient.astype(BF16)


def solution(mesh):
    return jax.shard_map(
        body,
        mesh=mesh,
        in_specs=(P(None, "slab", "tile", None), P(), P(), P("tile", None, None), P(), P()),
        out_specs=P(None, "slab", "tile", None),
        check_vma=False,
    )
```

```python
import functools
import math

import jax
import jax.numpy as jnp
import numpy as np
from jax import lax
from jax.experimental import pallas as pl
from jax.experimental.pallas import tpu as pltpu
from jax.sharding import PartitionSpec as P

F32 = jnp.float32
BF16 = jnp.bfloat16


def fourier_parts(window):
    index = np.arange(window)
    angle = (index[:, None] * index[None, :] % window) * (-2.0 * math.pi / window)
    real = np.cos(angle) / math.sqrt(window)
    imag = np.sin(angle) / math.sqrt(window)
    big = np.block([[real, imag], [-imag, real]]).astype(np.float32)
    high = big.astype(BF16)
    low = (big - high.astype(np.float32)).astype(BF16)
    right = np.concatenate([high, high, low], axis=0)
    left = np.concatenate([high.T, high.T, low.T], axis=1)
    return right, left


def split(value):
    high = value.astype(BF16)
    return high, (value - high.astype(F32)).astype(BF16)


def transform(field, right, left, window):
    count = len(field)
    high, low = split(
        jnp.concatenate([jnp.concatenate([re, im], axis=1) for re, im in field], axis=0)
    )
    first = jnp.dot(
        jnp.concatenate([high, low, high], axis=1), right[...], preferred_element_type=F32
    )
    rows = [first[p * window : (p + 1) * window] for p in range(count)]
    high, low = split(
        jnp.concatenate(
            [jnp.concatenate([r[:, :window], r[:, window:]], axis=0) for r in rows], axis=1
        )
    )
    second = jnp.dot(
        left[...], jnp.concatenate([high, low, high], axis=0), preferred_element_type=F32
    )
    out = []
    for p in range(count):
        block = second[:, p * window : (p + 1) * window]
        out.append((block[:window], block[window:]))
    return out


def times(a, b):
    return a[0] * b[0] - a[1] * b[1], a[0] * b[1] + a[1] * b[0]


def conj_times(a, b):
    return a[0] * b[0] + a[1] * b[1], a[0] * b[1] - a[1] * b[0]


def conj(a):
    return a[0], -a[1]


def load(ref, lead, count, window):
    out = []
    for p in range(count):
        block = ref[lead, p].astype(F32)
        out.append((block[:, :window], block[:, window:]))
    return out


def store(ref, lead, field):
    for p, (re, im) in enumerate(field):
        ref[lead, p] = jnp.concatenate([re, im], axis=1).astype(ref.dtype)


MESH = pl.DeviceIdType.MESH


def one_hot(shape, along, offset):
    here = lax.broadcasted_iota(jnp.int32, shape, along)
    there = lax.broadcasted_iota(jnp.int32, shape, 1 - along)
    return jnp.where(here == there + offset, 1.0, 0.0).astype(BF16)


def halves(block, window):
    return block[:, :window], block[:, window:]


def kernel(
    tiles, sections, row_ref, col_ref, obj, probe, phase, measured, right, left, out,
    cut_prior, cut_own, low, patches, psi, work, terms, spill, spilled,
    tile_send, tile_recv, cross_send, cross_recv, pair_send, pair_recv, back_send, back_recv,
):
    layers, window, columns = obj.shape[1], obj.shape[2], obj.shape[3]
    count, slices = measured.shape[0], patches.shape[0]
    groups = sections // 2
    last = slices - 1
    tile = lax.axis_index("tile")
    slab = lax.axis_index("slab")
    after, prior = lax.rem(tile + 1, tiles), lax.rem(tile + tiles - 1, tiles)
    group, side = slab // 2, lax.rem(slab, 2)
    partner = slab + 1 - 2 * side
    first_own = slab * layers

    def remote(src, dst, send, recv, **device):
        return pltpu.make_async_remote_copy(
            src_ref=src, dst_ref=dst, send_sem=send, recv_sem=recv,
            device_id=device, device_id_type=MESH,
        )

    barrier = pltpu.get_barrier_semaphore()
    greeted = [{"tile": after}, {"tile": prior}, {"slab": partner}]
    for step in range(1, groups):
        greeted.append({"slab": lax.rem(group + step, groups) * 2 + side})
    for device in greeted:
        pl.semaphore_signal(barrier, inc=1, device_id=device, device_id_type=MESH)

    def columns_of(base):
        return [col_ref[base * count + p] for p in range(count)]

    prior_cols, own_cols = columns_of(prior), columns_of(tile)
    own_rows = [row_ref[tile * count + p] for p in range(count)]

    def cut(cols, layer, target):
        pick = jnp.concatenate([one_hot((columns, window), 0, c) for c in cols], axis=1)
        both = jnp.concatenate([obj[0, layer], obj[1, layer]], axis=0)
        got = jnp.dot(both, pick, preferred_element_type=F32).astype(BF16)
        for p in range(count):
            part = got[:, p * window : (p + 1) * window]
            target[layer, p] = jnp.concatenate([part[:window], part[window:]], axis=1)

    def tile_copy(layer):
        return remote(
            cut_prior.at[layer], low.at[layer], tile_send.at[layer], tile_recv.at[layer], tile=prior
        )

    for layer in range(layers):
        cut(prior_cols, layer, cut_prior)
    pl.semaphore_wait(barrier, len(greeted))
    for layer in range(layers):
        tile_copy(layer).start()
    for layer in range(layers):
        cut(own_cols, layer, cut_own)
    work[count] = jnp.concatenate([jnp.cos(phase[...]), jnp.sin(phase[...])], axis=1)

    def cross_copy(step, layer):
        block = patches.at[first_own + layer]
        return remote(
            block, block, cross_send.at[step - 1, layer], cross_recv.at[step - 1, layer],
            slab=lax.rem(group + step, groups) * 2 + side,
        )

    def origin(step, of_side):
        return (lax.rem(group + groups - step, groups) * 2 + of_side) * layers

    def cross_arrival(step, layer):
        block = patches.at[origin(step, side) + layer]
        return remote(
            block, block, cross_send.at[step - 1, layer], cross_recv.at[step - 1, layer],
            slab=lax.rem(group + step, groups) * 2 + side,
        )

    def pair_copy(step, layer):
        block = patches.at[origin(step, side) + layer]
        return remote(
            block, block, pair_send.at[step, layer], pair_recv.at[step, layer], slab=partner
        )

    def pair_arrival(step, layer):
        block = patches.at[origin(step, 1 - side) + layer]
        return remote(
            block, block, pair_send.at[step, layer], pair_recv.at[step, layer], slab=partner
        )

    for layer in range(layers):
        tile_copy(layer).wait_recv()
        for p in range(count):
            both = jnp.concatenate([cut_own[layer, p], low[layer, p]], axis=0)
            pick = one_hot((window, 2 * window), 1, own_rows[p])
            patches[first_own + layer, p] = jnp.dot(
                pick, both, preferred_element_type=F32
            ).astype(BF16)
        for step in range(1, groups):
            cross_copy(step, layer).start()
        pair_copy(0, layer).start()
    for layer in range(layers):
        for step in range(1, groups):
            cross_arrival(step, layer).wait_recv()
            pair_copy(step, layer).start()
    for layer in range(layers):
        for step in range(groups):
            pair_arrival(step, layer).wait_recv()

    run = functools.partial(transform, right=right, left=left, window=window)
    start = (probe[0].astype(F32), probe[1].astype(F32))
    store(psi, 0, [start] * count)

    def propagator():
        return halves(work[count], window)

    def forward(j, carried):
        chi = [
            times(a, b)
            for a, b in zip(load(psi, j, count, window), load(patches, j, count, window))
        ]
        moved = run(chi)
        prop = propagator()
        back = run([conj(times(prop, f)) for f in moved])
        store(psi, j + 1, [conj(f) for f in back])
        return carried

    lax.fori_loop(0, last, forward, 0)
    chi = [
        times(a, b)
        for a, b in zip(load(psi, last, count, window), load(patches, last, count, window))
    ]
    far = run(chi)
    shaped = []
    for p, (re, im) in enumerate(far):
        misfit = re * re + im * im - measured[p]
        shaped.append((misfit * re, -(misfit * im)))
    grad = [conj(f) for f in run(shaped)]
    for p in range(count):
        work[p] = jnp.concatenate(grad[p], axis=1)

    def spill_copy(layer):
        return remote(
            spill.at[layer], spilled.at[layer], back_send.at[layer], back_recv.at[layer], tile=after
        )

    def own_term(j):
        @pl.when((j >= first_own) & (j < first_own + layers))
        def _():
            layer = j - first_own
            for p in range(count):
                term = jnp.concatenate(
                    conj_times(halves(psi[j, p], window), halves(work[p], window)), axis=1
                )
                pick = one_hot((2 * window, window), 0, own_rows[p])
                placed = jnp.dot(
                    jnp.concatenate([pick, pick], axis=1),
                    jnp.concatenate(split(term), axis=0),
                    preferred_element_type=F32,
                )
                terms[layer, p] = placed[:window]
                spill[layer, p] = placed[window:].astype(BF16)
            spill_copy(layer).start()

    def backward(i, carried):
        j = last - i
        own_term(j)
        grads = [halves(work[p], window) for p in range(count)]
        inner = [conj_times(a, b) for a, b in zip(load(patches, j, count, window), grads)]
        moved = run(inner)
        prop = propagator()
        back = run([conj(conj_times(prop, f)) for f in moved])
        for p in range(count):
            work[p] = jnp.concatenate(conj(back[p]), axis=1)
        return carried

    lax.fori_loop(0, last, backward, 0)
    own_term(0)

    own_place = jnp.concatenate([one_hot((window, columns), 1, c) for c in own_cols], axis=0)
    prior_place = jnp.concatenate([one_hot((window, columns), 1, c) for c in prior_cols], axis=0)

    def by_part(ref, layer):
        wide = [halves(ref[layer, p], window) for p in range(count)]
        return jnp.concatenate(
            [jnp.concatenate([w[part] for w in wide], axis=1) for part in range(2)], axis=0
        )

    for layer in reversed(range(layers)):
        high, low_part = split(by_part(terms, layer))
        total = jnp.dot(high, own_place, preferred_element_type=F32)
        total += jnp.dot(low_part, own_place, preferred_element_type=F32)
        spill_copy(layer).wait_recv()
        total += jnp.dot(by_part(spilled, layer), prior_place, preferred_element_type=F32)
        out[0, layer] = total[:window].astype(out.dtype)
        out[1, layer] = total[window:].astype(out.dtype)
    for layer in range(layers):
        tile_copy(layer).wait_send()
        spill_copy(layer).wait_send()
        for step in range(1, groups):
            cross_copy(step, layer).wait_send()
        for step in range(groups):
            pair_copy(step, layer).wait_send()


def body(object_field, probe_wave, prop_phase, intensity, patch_rows, patch_cols):
    window = probe_wave.shape[1]
    layers = object_field.shape[1]
    count = intensity.shape[0]
    tiles, sections = lax.axis_size("tile"), lax.axis_size("slab")
    slices = sections * layers
    groups = sections // 2
    right, left = fourier_parts(window)
    wide = (layers, count, window, 2 * window)
    dma = pltpu.SemaphoreType.DMA
    return pl.pallas_call(
        functools.partial(kernel, tiles, sections),
        out_shape=jax.ShapeDtypeStruct(object_field.shape, BF16),
        in_specs=[pl.BlockSpec(memory_space=pltpu.SMEM)] * 2
        + [pl.BlockSpec(memory_space=pltpu.VMEM)] * 6,
        out_specs=pl.BlockSpec(memory_space=pltpu.VMEM),
        scratch_shapes=[
            pltpu.VMEM(wide, BF16),
            pltpu.VMEM(wide, BF16),
            pltpu.VMEM(wide, BF16),
            pltpu.VMEM((slices,) + wide[1:], BF16),
            pltpu.VMEM((slices,) + wide[1:], F32),
            pltpu.VMEM((count + 1, window, 2 * window), F32),
            pltpu.VMEM(wide, F32),
            pltpu.VMEM(wide, BF16),
            pltpu.VMEM(wide, BF16),
            dma((layers,)),
            dma((layers,)),
            dma((groups - 1, layers)),
            dma((groups - 1, layers)),
            dma((groups, layers)),
            dma((groups, layers)),
            dma((layers,)),
            dma((layers,)),
        ],
        compiler_params=pltpu.CompilerParams(
            collective_id=0, has_side_effects=True, vmem_limit_bytes=60 * 1024 * 1024
        ),
    )(
        patch_rows, patch_cols, object_field, probe_wave, prop_phase, intensity,
        jnp.asarray(right), jnp.asarray(left),
    )


def solution(mesh):
    return jax.shard_map(
        body,
        mesh=mesh,
        in_specs=(P(None, "slab", "tile", None), P(), P(), P("tile", None, None), P(), P()),
        out_specs=P(None, "slab", "tile", None),
        check_vma=False,
    )
```

```python
import functools
import math

import jax
import jax.numpy as jnp
import numpy as np
from jax import lax
from jax.experimental import pallas as pl
from jax.experimental.pallas import tpu as pltpu
from jax.sharding import PartitionSpec as P

F32 = jnp.float32
BF16 = jnp.bfloat16


def fourier_parts(window):
    index = np.arange(window)
    angle = (index[:, None] * index[None, :] % window) * (-2.0 * math.pi / window)
    real = np.cos(angle) / math.sqrt(window)
    imag = np.sin(angle) / math.sqrt(window)
    big = np.block([[real, imag], [-imag, real]]).astype(np.float32)
    high = big.astype(BF16)
    low = (big - high.astype(np.float32)).astype(BF16)
    right = np.concatenate([high, high, low], axis=0)
    left = np.concatenate([high.T, high.T, low.T], axis=1)
    return right, left


def split(value):
    high = value.astype(BF16)
    return high, (value - high.astype(F32)).astype(BF16)


def transform(field, right, left, window):
    count = len(field)
    high, low = split(
        jnp.concatenate([jnp.concatenate([re, im], axis=1) for re, im in field], axis=0)
    )
    first = jnp.dot(
        jnp.concatenate([high, low, high], axis=1), right[...], preferred_element_type=F32
    )
    rows = [first[p * window : (p + 1) * window] for p in range(count)]
    high, low = split(
        jnp.concatenate(
            [jnp.concatenate([r[:, :window], r[:, window:]], axis=0) for r in rows], axis=1
        )
    )
    second = jnp.dot(
        left[...], jnp.concatenate([high, low, high], axis=0), preferred_element_type=F32
    )
    out = []
    for p in range(count):
        block = second[:, p * window : (p + 1) * window]
        out.append((block[:window], block[window:]))
    return out


def times(a, b):
    return a[0] * b[0] - a[1] * b[1], a[0] * b[1] + a[1] * b[0]


def conj_times(a, b):
    return a[0] * b[0] + a[1] * b[1], a[0] * b[1] - a[1] * b[0]


def conj(a):
    return a[0], -a[1]


def load(ref, lead, count, window):
    out = []
    for p in range(count):
        block = ref[lead, p].astype(F32)
        out.append((block[:, :window], block[:, window:]))
    return out


def store(ref, lead, field):
    for p, (re, im) in enumerate(field):
        ref[lead, p] = jnp.concatenate([re, im], axis=1).astype(ref.dtype)


MESH = pl.DeviceIdType.MESH


def one_hot(shape, along, offset):
    here = lax.broadcasted_iota(jnp.int32, shape, along)
    there = lax.broadcasted_iota(jnp.int32, shape, 1 - along)
    return jnp.where(here == there + offset, 1.0, 0.0).astype(BF16)


def halves(block, window):
    return block[:, :window], block[:, window:]


def kernel(
    tiles, sections, row_ref, col_ref, obj, probe, phase, measured, right, left, out,
    cut_prior, cut_own, low, patches, psi, work, terms, spill, spilled,
    tile_send, tile_recv, cross_send, cross_recv, pair_send, pair_recv, back_send, back_recv,
):
    layers, window, columns = obj.shape[1], obj.shape[2], obj.shape[3]
    count, slices = measured.shape[0], patches.shape[0]
    groups = sections // 2
    last = slices - 1
    tile = lax.axis_index("tile")
    slab = lax.axis_index("slab")
    after, prior = lax.rem(tile + 1, tiles), lax.rem(tile + tiles - 1, tiles)
    group, side = slab // 2, lax.rem(slab, 2)
    partner = slab + 1 - 2 * side
    first_own = slab * layers

    def remote(src, dst, send, recv, **device):
        return pltpu.make_async_remote_copy(
            src_ref=src, dst_ref=dst, send_sem=send, recv_sem=recv,
            device_id=device, device_id_type=MESH,
        )

    barrier = pltpu.get_barrier_semaphore()
    greeted = [{"tile": after}, {"tile": prior}, {"slab": partner}]
    for step in range(1, groups):
        greeted.append({"slab": lax.rem(group + step, groups) * 2 + side})
    for device in greeted:
        pl.semaphore_signal(barrier, inc=1, device_id=device, device_id_type=MESH)

    def columns_of(base):
        return [col_ref[base * count + p] for p in range(count)]

    prior_cols, own_cols = columns_of(prior), columns_of(tile)
    own_rows = [row_ref[tile * count + p] for p in range(count)]

    def cut(cols, layer, target):
        pick = jnp.concatenate([one_hot((columns, window), 0, c) for c in cols], axis=1)
        both = jnp.concatenate([obj[0, layer], obj[1, layer]], axis=0)
        got = jnp.dot(both, pick, preferred_element_type=F32).astype(BF16)
        for p in range(count):
            part = got[:, p * window : (p + 1) * window]
            target[layer, p] = jnp.concatenate([part[:window], part[window:]], axis=1)

    def tile_copy(layer):
        return remote(
            cut_prior.at[layer], low.at[layer], tile_send.at[layer], tile_recv.at[layer], tile=prior
        )

    for layer in range(layers):
        cut(prior_cols, layer, cut_prior)
    pl.semaphore_wait(barrier, len(greeted))
    for layer in range(layers):
        tile_copy(layer).start()
    for layer in range(layers):
        cut(own_cols, layer, cut_own)
    work[count] = jnp.concatenate([jnp.cos(phase[...]), jnp.sin(phase[...])], axis=1)

    def cross_copy(step, layer):
        block = patches.at[first_own + layer]
        return remote(
            block, block, cross_send.at[step - 1, layer], cross_recv.at[step - 1, layer],
            slab=lax.rem(group + step, groups) * 2 + side,
        )

    def origin(step, of_side):
        return (lax.rem(group + groups - step, groups) * 2 + of_side) * layers

    def cross_arrival(step, layer):
        block = patches.at[origin(step, side) + layer]
        return remote(
            block, block, cross_send.at[step - 1, layer], cross_recv.at[step - 1, layer],
            slab=lax.rem(group + step, groups) * 2 + side,
        )

    def pair_copy(step, layer):
        block = patches.at[origin(step, side) + layer]
        return remote(
            block, block, pair_send.at[step, layer], pair_recv.at[step, layer], slab=partner
        )

    def pair_arrival(step, layer):
        block = patches.at[origin(step, 1 - side) + layer]
        return remote(
            block, block, pair_send.at[step, layer], pair_recv.at[step, layer], slab=partner
        )

    def take_rows(layer):
        tile_copy(layer).wait_recv()
        for p in range(count):
            both = jnp.concatenate([cut_own[layer, p], low[layer, p]], axis=0)
            pick = one_hot((window, 2 * window), 1, own_rows[p])
            patches[first_own + layer, p] = jnp.dot(
                pick, both, preferred_element_type=F32
            ).astype(BF16)
        pair_copy(0, layer).start()
        for step in range(1, groups):
            cross_copy(step, layer).start()

    take_rows(0)

    @pl.when(group > 0)
    def _():
        for layer in range(1, layers):
            take_rows(layer)

    def arrive(j):
        owner, layer = j // layers, lax.rem(j, layers)
        of_group, of_side = owner // 2, lax.rem(owner, 2)
        step = lax.rem(group - of_group + groups, groups)

        @pl.when((of_side == side) & (of_group != group))
        def _():
            cross_arrival(step, layer).wait_recv()
            pair_copy(step, layer).start()

        @pl.when(of_side != side)
        def _():
            pair_arrival(step, layer).wait_recv()

    run = functools.partial(transform, right=right, left=left, window=window)
    start = (probe[0].astype(F32), probe[1].astype(F32))
    store(psi, 0, [start] * count)

    def propagator():
        return halves(work[count], window)

    def forward(j, carried):
        @pl.when((group == 0) & (j >= 1) & (j < layers))
        def _():
            take_rows(j)

        arrive(j)
        chi = [
            times(a, b)
            for a, b in zip(load(psi, j, count, window), load(patches, j, count, window))
        ]
        moved = run(chi)
        prop = propagator()
        back = run([conj(times(prop, f)) for f in moved])
        store(psi, j + 1, [conj(f) for f in back])
        return carried

    lax.fori_loop(0, last, forward, 0)
    arrive(last)
    chi = [
        times(a, b)
        for a, b in zip(load(psi, last, count, window), load(patches, last, count, window))
    ]
    far = run(chi)
    shaped = []
    for p, (re, im) in enumerate(far):
        misfit = re * re + im * im - measured[p]
        shaped.append((misfit * re, -(misfit * im)))
    grad = [conj(f) for f in run(shaped)]
    for p in range(count):
        work[p] = jnp.concatenate(grad[p], axis=1)

    def spill_copy(layer):
        return remote(
            spill.at[layer], spilled.at[layer], back_send.at[layer], back_recv.at[layer], tile=after
        )

    def own_term(j):
        @pl.when((j >= first_own) & (j < first_own + layers))
        def _():
            layer = j - first_own
            for p in range(count):
                term = jnp.concatenate(
                    conj_times(halves(psi[j, p], window), halves(work[p], window)), axis=1
                )
                pick = one_hot((2 * window, window), 0, own_rows[p])
                placed = jnp.dot(
                    jnp.concatenate([pick, pick], axis=1),
                    jnp.concatenate(split(term), axis=0),
                    preferred_element_type=F32,
                )
                terms[layer, p] = placed[:window]
                spill[layer, p] = placed[window:].astype(BF16)
            spill_copy(layer).start()

    def backward(i, carried):
        j = last - i
        own_term(j)
        grads = [halves(work[p], window) for p in range(count)]
        inner = [conj_times(a, b) for a, b in zip(load(patches, j, count, window), grads)]
        moved = run(inner)
        prop = propagator()
        back = run([conj(conj_times(prop, f)) for f in moved])
        for p in range(count):
            work[p] = jnp.concatenate(conj(back[p]), axis=1)
        return carried

    lax.fori_loop(0, last - first_own, backward, 0)
    own_term(first_own)

    own_place = jnp.concatenate([one_hot((window, columns), 1, c) for c in own_cols], axis=0)
    prior_place = jnp.concatenate([one_hot((window, columns), 1, c) for c in prior_cols], axis=0)

    def by_part(ref, layer):
        wide = [halves(ref[layer, p], window) for p in range(count)]
        return jnp.concatenate(
            [jnp.concatenate([w[part] for w in wide], axis=1) for part in range(2)], axis=0
        )

    for layer in reversed(range(layers)):
        high, low_part = split(by_part(terms, layer))
        total = jnp.dot(high, own_place, preferred_element_type=F32)
        total += jnp.dot(low_part, own_place, preferred_element_type=F32)
        spill_copy(layer).wait_recv()
        total += jnp.dot(by_part(spilled, layer), prior_place, preferred_element_type=F32)
        out[0, layer] = total[:window].astype(out.dtype)
        out[1, layer] = total[window:].astype(out.dtype)
    for layer in range(layers):
        tile_copy(layer).wait_send()
        spill_copy(layer).wait_send()
        for step in range(1, groups):
            cross_copy(step, layer).wait_send()
        for step in range(groups):
            pair_copy(step, layer).wait_send()


def body(object_field, probe_wave, prop_phase, intensity, patch_rows, patch_cols):
    window = probe_wave.shape[1]
    layers = object_field.shape[1]
    count = intensity.shape[0]
    tiles, sections = lax.axis_size("tile"), lax.axis_size("slab")
    slices = sections * layers
    groups = sections // 2
    right, left = fourier_parts(window)
    wide = (layers, count, window, 2 * window)
    dma = pltpu.SemaphoreType.DMA
    return pl.pallas_call(
        functools.partial(kernel, tiles, sections),
        out_shape=jax.ShapeDtypeStruct(object_field.shape, BF16),
        in_specs=[pl.BlockSpec(memory_space=pltpu.SMEM)] * 2
        + [pl.BlockSpec(memory_space=pltpu.VMEM)] * 6,
        out_specs=pl.BlockSpec(memory_space=pltpu.VMEM),
        scratch_shapes=[
            pltpu.VMEM(wide, BF16),
            pltpu.VMEM(wide, BF16),
            pltpu.VMEM(wide, BF16),
            pltpu.VMEM((slices,) + wide[1:], BF16),
            pltpu.VMEM((slices,) + wide[1:], F32),
            pltpu.VMEM((count + 1, window, 2 * window), F32),
            pltpu.VMEM(wide, F32),
            pltpu.VMEM(wide, BF16),
            pltpu.VMEM(wide, BF16),
            dma((layers,)),
            dma((layers,)),
            dma((groups - 1, layers)),
            dma((groups - 1, layers)),
            dma((groups, layers)),
            dma((groups, layers)),
            dma((layers,)),
            dma((layers,)),
        ],
        compiler_params=pltpu.CompilerParams(
            collective_id=0, has_side_effects=True, vmem_limit_bytes=60 * 1024 * 1024
        ),
    )(
        patch_rows, patch_cols, object_field, probe_wave, prop_phase, intensity,
        jnp.asarray(right), jnp.asarray(left),
    )


def solution(mesh):
    return jax.shard_map(
        body,
        mesh=mesh,
        in_specs=(P(None, "slab", "tile", None), P(), P(), P("tile", None, None), P(), P()),
        out_specs=P(None, "slab", "tile", None),
        check_vma=False,
    )
```

```python
import functools
import math

import jax
import jax.numpy as jnp
import numpy as np
from jax import lax
from jax.experimental import pallas as pl
from jax.experimental.pallas import tpu as pltpu
from jax.sharding import PartitionSpec as P

F32 = jnp.float32
BF16 = jnp.bfloat16


def fourier_parts(window):
    index = np.arange(window)
    angle = (index[:, None] * index[None, :] % window) * (-2.0 * math.pi / window)
    real = np.cos(angle) / math.sqrt(window)
    imag = np.sin(angle) / math.sqrt(window)
    big = np.block([[real, imag], [-imag, real]]).astype(np.float32)
    high = big.astype(BF16)
    low = (big - high.astype(np.float32)).astype(BF16)
    return np.concatenate([high, high, low], axis=0)


def split(value):
    high = value.astype(BF16)
    return high, (value - high.astype(F32)).astype(BF16)


def from_right(field, right, window):
    high, low = split(jnp.concatenate(field, axis=1))
    product = jnp.dot(
        jnp.concatenate([high, low, high], axis=1), right[...], preferred_element_type=F32
    )
    return product[:, :window], product[:, window:]


def transform(field, right, window):
    first = [from_right(f, right, window) for f in field]
    return [from_right((re.T, im.T), right, window) for re, im in first]


def times(a, b):
    return a[0] * b[0] - a[1] * b[1], a[0] * b[1] + a[1] * b[0]


def conj_times(a, b):
    return a[0] * b[0] + a[1] * b[1], a[0] * b[1] - a[1] * b[0]


def conj(a):
    return a[0], -a[1]


def load(ref, lead, count, window):
    out = []
    for p in range(count):
        block = ref[lead, p].astype(F32)
        out.append((block[:, :window], block[:, window:]))
    return out


def store(ref, lead, field):
    for p, (re, im) in enumerate(field):
        ref[lead, p] = jnp.concatenate([re, im], axis=1).astype(ref.dtype)


MESH = pl.DeviceIdType.MESH


def one_hot(shape, along, offset):
    here = lax.broadcasted_iota(jnp.int32, shape, along)
    there = lax.broadcasted_iota(jnp.int32, shape, 1 - along)
    return jnp.where(here == there + offset, 1.0, 0.0).astype(BF16)


def halves(block, window):
    return block[:, :window], block[:, window:]


def kernel(
    tiles, sections, row_ref, col_ref, obj, probe, phase, measured, right_in, out,
    cut_prior, cut_own, low, patches, psi, work, terms, spill, spilled, right, turned,
    tile_send, tile_recv, cross_send, cross_recv, pair_send, pair_recv, back_send, back_recv, table_sem,
):
    layers, window, columns = obj.shape[1], obj.shape[2], obj.shape[3]
    count, slices = measured.shape[0], patches.shape[0]
    groups = sections // 2
    last = slices - 1
    tile = lax.axis_index("tile")
    slab = lax.axis_index("slab")
    after, prior = lax.rem(tile + 1, tiles), lax.rem(tile + tiles - 1, tiles)
    group, side = slab // 2, lax.rem(slab, 2)
    partner = slab + 1 - 2 * side
    first_own = slab * layers

    def remote(src, dst, send, recv, **device):
        return pltpu.make_async_remote_copy(
            src_ref=src, dst_ref=dst, send_sem=send, recv_sem=recv,
            device_id=device, device_id_type=MESH,
        )

    table = pltpu.make_async_copy(right_in, right, table_sem)
    table.start()
    barrier = pltpu.get_barrier_semaphore()
    greeted = [{"tile": after}, {"tile": prior}, {"slab": partner}]
    for step in range(1, groups):
        greeted.append({"slab": lax.rem(group + step, groups) * 2 + side})
    for device in greeted:
        pl.semaphore_signal(barrier, inc=1, device_id=device, device_id_type=MESH)

    def columns_of(base):
        return [col_ref[base * count + p] for p in range(count)]

    prior_cols, own_cols = columns_of(prior), columns_of(tile)
    own_rows = [row_ref[tile * count + p] for p in range(count)]

    def cut(cols, layer, target):
        pick = jnp.concatenate([one_hot((columns, window), 0, c) for c in cols], axis=1)
        both = jnp.concatenate([obj[0, layer], obj[1, layer]], axis=0)
        got = jnp.dot(both, pick, preferred_element_type=F32).astype(BF16)
        for p in range(count):
            part = got[:, p * window : (p + 1) * window]
            target[layer, p] = jnp.concatenate([part[:window], part[window:]], axis=1)

    def tile_copy(layer):
        return remote(
            cut_prior.at[layer], low.at[layer], tile_send.at[layer], tile_recv.at[layer], tile=prior
        )

    for layer in range(layers):
        cut(prior_cols, layer, cut_prior)
    pl.semaphore_wait(barrier, len(greeted))
    for layer in range(layers):
        tile_copy(layer).start()
    for layer in range(layers):
        cut(own_cols, layer, cut_own)
    phase_turned = phase[...].T
    work[count] = jnp.concatenate([jnp.cos(phase_turned), jnp.sin(phase_turned)], axis=1)
    for p in range(count):
        turned[p] = measured[p].T

    def cross_copy(step, layer):
        block = patches.at[first_own + layer]
        return remote(
            block, block, cross_send.at[step - 1, layer], cross_recv.at[step - 1, layer],
            slab=lax.rem(group + step, groups) * 2 + side,
        )

    def origin(step, of_side):
        return (lax.rem(group + groups - step, groups) * 2 + of_side) * layers

    def cross_arrival(step, layer):
        block = patches.at[origin(step, side) + layer]
        return remote(
            block, block, cross_send.at[step - 1, layer], cross_recv.at[step - 1, layer],
            slab=lax.rem(group + step, groups) * 2 + side,
        )

    def pair_copy(step, layer):
        block = patches.at[origin(step, side) + layer]
        return remote(
            block, block, pair_send.at[step, layer], pair_recv.at[step, layer], slab=partner
        )

    def pair_arrival(step, layer):
        block = patches.at[origin(step, 1 - side) + layer]
        return remote(
            block, block, pair_send.at[step, layer], pair_recv.at[step, layer], slab=partner
        )

    def take_rows(layer):
        tile_copy(layer).wait_recv()
        for p in range(count):
            both = jnp.concatenate([cut_own[layer, p], low[layer, p]], axis=0)
            pick = one_hot((window, 2 * window), 1, own_rows[p])
            patches[first_own + layer, p] = jnp.dot(
                pick, both, preferred_element_type=F32
            ).astype(BF16)
        pair_copy(0, layer).start()
        for step in range(1, groups):
            cross_copy(step, layer).start()

    take_rows(0)

    @pl.when(group > 0)
    def _():
        for layer in range(1, layers):
            take_rows(layer)

    def arrive(j):
        owner, layer = j // layers, lax.rem(j, layers)
        of_group, of_side = owner // 2, lax.rem(owner, 2)
        step = lax.rem(group - of_group + groups, groups)

        @pl.when((of_side == side) & (of_group != group))
        def _():
            cross_arrival(step, layer).wait_recv()
            pair_copy(step, layer).start()

        @pl.when(of_side != side)
        def _():
            pair_arrival(step, layer).wait_recv()

    table.wait()
    run = functools.partial(transform, right=right, window=window)
    start = (probe[0].astype(F32), probe[1].astype(F32))
    store(psi, 0, [start] * count)

    def propagator():
        return halves(work[count], window)

    def forward(j, carried):
        @pl.when((group == 0) & (j >= 1) & (j < layers))
        def _():
            take_rows(j)

        arrive(j)
        chi = [
            times(a, b)
            for a, b in zip(load(psi, j, count, window), load(patches, j, count, window))
        ]
        moved = run(chi)
        prop = propagator()
        back = run([conj(times(prop, f)) for f in moved])
        store(psi, j + 1, [conj(f) for f in back])
        return carried

    lax.fori_loop(0, last, forward, 0)
    arrive(last)
    chi = [
        times(a, b)
        for a, b in zip(load(psi, last, count, window), load(patches, last, count, window))
    ]
    far = run(chi)
    shaped = []
    for p, (re, im) in enumerate(far):
        misfit = re * re + im * im - turned[p]
        shaped.append((misfit * re, -(misfit * im)))
    grad = [conj(f) for f in run(shaped)]
    for p in range(count):
        work[p] = jnp.concatenate(grad[p], axis=1)

    def spill_copy(layer):
        return remote(
            spill.at[layer], spilled.at[layer], back_send.at[layer], back_recv.at[layer], tile=after
        )

    def own_term(j):
        @pl.when((j >= first_own) & (j < first_own + layers))
        def _():
            layer = j - first_own
            for p in range(count):
                term = jnp.concatenate(
                    conj_times(halves(psi[j, p], window), halves(work[p], window)), axis=1
                )
                pick = one_hot((2 * window, window), 0, own_rows[p])
                placed = jnp.dot(
                    jnp.concatenate([pick, pick], axis=1),
                    jnp.concatenate(split(term), axis=0),
                    preferred_element_type=F32,
                )
                terms[layer, p] = placed[:window]
                spill[layer, p] = placed[window:].astype(BF16)
            spill_copy(layer).start()

    def backward(i, carried):
        j = last - i
        own_term(j)
        grads = [halves(work[p], window) for p in range(count)]
        inner = [conj_times(a, b) for a, b in zip(load(patches, j, count, window), grads)]
        moved = run(inner)
        prop = propagator()
        back = run([conj(conj_times(prop, f)) for f in moved])
        for p in range(count):
            work[p] = jnp.concatenate(conj(back[p]), axis=1)
        return carried

    lax.fori_loop(0, last - first_own, backward, 0)
    own_term(first_own)

    own_place = jnp.concatenate([one_hot((window, columns), 1, c) for c in own_cols], axis=0)
    prior_place = jnp.concatenate([one_hot((window, columns), 1, c) for c in prior_cols], axis=0)

    def by_part(ref, layer):
        wide = [halves(ref[layer, p], window) for p in range(count)]
        return jnp.concatenate(
            [jnp.concatenate([w[part] for w in wide], axis=1) for part in range(2)], axis=0
        )

    for layer in reversed(range(layers)):
        high, low_part = split(by_part(terms, layer))
        total = jnp.dot(high, own_place, preferred_element_type=F32)
        total += jnp.dot(low_part, own_place, preferred_element_type=F32)
        spill_copy(layer).wait_recv()
        total += jnp.dot(by_part(spilled, layer), prior_place, preferred_element_type=F32)
        out[0, layer] = total[:window].astype(out.dtype)
        out[1, layer] = total[window:].astype(out.dtype)
    for layer in range(layers):
        tile_copy(layer).wait_send()
        spill_copy(layer).wait_send()
        for step in range(1, groups):
            cross_copy(step, layer).wait_send()
        for step in range(groups):
            pair_copy(step, layer).wait_send()


def body(object_field, probe_wave, prop_phase, intensity, patch_rows, patch_cols):
    window = probe_wave.shape[1]
    layers = object_field.shape[1]
    count = intensity.shape[0]
    tiles, sections = lax.axis_size("tile"), lax.axis_size("slab")
    slices = sections * layers
    groups = sections // 2
    right = fourier_parts(window)
    wide = (layers, count, window, 2 * window)
    dma = pltpu.SemaphoreType.DMA
    return pl.pallas_call(
        functools.partial(kernel, tiles, sections),
        out_shape=jax.ShapeDtypeStruct(object_field.shape, BF16),
        in_specs=[pl.BlockSpec(memory_space=pltpu.SMEM)] * 2
        + [pl.BlockSpec(memory_space=pltpu.VMEM)] * 4
        + [pl.BlockSpec(memory_space=pl.ANY)],
        out_specs=pl.BlockSpec(memory_space=pltpu.VMEM),
        scratch_shapes=[
            pltpu.VMEM(wide, BF16),
            pltpu.VMEM(wide, BF16),
            pltpu.VMEM(wide, BF16),
            pltpu.VMEM((slices,) + wide[1:], BF16),
            pltpu.VMEM((slices,) + wide[1:], F32),
            pltpu.VMEM((count + 1, window, 2 * window), F32),
            pltpu.VMEM(wide, F32),
            pltpu.VMEM(wide, BF16),
            pltpu.VMEM(wide, BF16),
            pltpu.VMEM(right.shape, BF16),
            pltpu.VMEM(intensity.shape, F32),
            dma((layers,)),
            dma((layers,)),
            dma((groups - 1, layers)),
            dma((groups - 1, layers)),
            dma((groups, layers)),
            dma((groups, layers)),
            dma((layers,)),
            dma((layers,)),
            dma(()),
        ],
        compiler_params=pltpu.CompilerParams(
            collective_id=0, has_side_effects=True, vmem_limit_bytes=60 * 1024 * 1024
        ),
    )(
        patch_rows, patch_cols, object_field, probe_wave, prop_phase, intensity,
        jnp.asarray(right),
    )


def solution(mesh):
    return jax.shard_map(
        body,
        mesh=mesh,
        in_specs=(P(None, "slab", "tile", None), P(), P(), P("tile", None, None), P(), P()),
        out_specs=P(None, "slab", "tile", None),
        check_vma=False,
    )
```

```python
import functools
import math

import jax
import jax.numpy as jnp
import numpy as np
from jax import lax
from jax.experimental import pallas as pl
from jax.experimental.pallas import tpu as pltpu
from jax.sharding import PartitionSpec as P

F32 = jnp.float32
BF16 = jnp.bfloat16


def fourier_parts(window):
    index = np.arange(window)
    angle = (index[:, None] * index[None, :] % window) * (-2.0 * math.pi / window)
    real = np.cos(angle) / math.sqrt(window)
    imag = np.sin(angle) / math.sqrt(window)
    big = np.block([[real, imag], [-imag, real]]).astype(np.float32)
    high = big.astype(BF16)
    low = (big - high.astype(np.float32)).astype(BF16)
    return np.concatenate([high, high, low], axis=0)


def split(value):
    high = value.astype(BF16)
    return high, (value - high.astype(F32)).astype(BF16)


def from_right(field, right, window):
    high, low = split(jnp.concatenate(field, axis=1))
    product = jnp.dot(
        jnp.concatenate([high, low, high], axis=1), right[...], preferred_element_type=F32
    )
    return product[:, :window], product[:, window:]


def transform(field, right, window):
    first = [from_right(f, right, window) for f in field]
    return [from_right((re.T, im.T), right, window) for re, im in first]


def times(a, b):
    return a[0] * b[0] - a[1] * b[1], a[0] * b[1] + a[1] * b[0]


def conj_times(a, b):
    return a[0] * b[0] + a[1] * b[1], a[0] * b[1] - a[1] * b[0]


def conj(a):
    return a[0], -a[1]


def load(ref, lead, count, window):
    out = []
    for p in range(count):
        block = ref[lead, p].astype(F32)
        out.append((block[:, :window], block[:, window:]))
    return out


def store(ref, lead, field):
    for p, (re, im) in enumerate(field):
        ref[lead, p] = jnp.concatenate([re, im], axis=1).astype(ref.dtype)


MESH = pl.DeviceIdType.MESH


def one_hot(shape, along, offset):
    here = lax.broadcasted_iota(jnp.int32, shape, along)
    there = lax.broadcasted_iota(jnp.int32, shape, 1 - along)
    return jnp.where(here == there + offset, 1.0, 0.0).astype(BF16)


def halves(block, window):
    return block[:, :window], block[:, window:]


def kernel(
    tiles, sections, row_ref, col_ref, obj, probe, phase, measured, right_in, out,
    cut_prior, cut_own, low, patches, psi, work, terms, spill, spilled, right, turned,
    tile_send, tile_recv, cross_send, cross_recv, pair_send, pair_recv, back_send, back_recv, table_sem, go,
):
    layers, window, columns = obj.shape[1], obj.shape[2], obj.shape[3]
    count, slices = measured.shape[0], patches.shape[0]
    groups = sections // 2
    last = slices - 1
    tile = lax.axis_index("tile")
    slab = lax.axis_index("slab")
    after, prior = lax.rem(tile + 1, tiles), lax.rem(tile + tiles - 1, tiles)
    group, side = slab // 2, lax.rem(slab, 2)
    partner = slab + 1 - 2 * side
    first_own = slab * layers

    def remote(src, dst, send, recv, **device):
        return pltpu.make_async_remote_copy(
            src_ref=src, dst_ref=dst, send_sem=send, recv_sem=recv,
            device_id=device, device_id_type=MESH,
        )

    table = pltpu.make_async_copy(right_in, right, table_sem)
    table.start()
    barrier = pltpu.get_barrier_semaphore()
    greeted = [{"tile": after}, {"tile": prior}, {"slab": partner}]
    for step in range(1, groups):
        greeted.append({"slab": lax.rem(group + step, groups) * 2 + side})
    for device in greeted:
        pl.semaphore_signal(barrier, inc=1, device_id=device, device_id_type=MESH)

    def columns_of(base):
        return [col_ref[base * count + p] for p in range(count)]

    prior_cols, own_cols = columns_of(prior), columns_of(tile)
    own_rows = [row_ref[tile * count + p] for p in range(count)]

    def cut(cols, layer, target):
        pick = jnp.concatenate([one_hot((columns, window), 0, c) for c in cols], axis=1)
        both = jnp.concatenate([obj[0, layer], obj[1, layer]], axis=0)
        got = jnp.dot(both, pick, preferred_element_type=F32).astype(BF16)
        for p in range(count):
            part = got[:, p * window : (p + 1) * window]
            target[layer, p] = jnp.concatenate([part[:window], part[window:]], axis=1)

    def tile_copy(layer):
        return remote(
            cut_prior.at[layer], low.at[layer], tile_send.at[layer], tile_recv.at[layer], tile=prior
        )

    for layer in range(layers):
        cut(prior_cols, layer, cut_prior)
    pl.semaphore_wait(barrier, len(greeted))

    @pl.when(side == 0)
    def _():
        for layer in range(layers):
            tile_copy(layer).start()

    for layer in range(layers):
        cut(own_cols, layer, cut_own)
    phase_turned = phase[...].T
    work[count] = jnp.concatenate([jnp.cos(phase_turned), jnp.sin(phase_turned)], axis=1)
    for p in range(count):
        turned[p] = measured[p].T

    @pl.when(side == 0)
    def _():
        for layer in range(layers):
            tile_copy(layer).wait_send()
        pl.semaphore_signal(go, inc=1, device_id={"slab": partner}, device_id_type=MESH)

    @pl.when(side == 1)
    def _():
        pl.semaphore_wait(go, 1)
        for layer in range(layers):
            tile_copy(layer).start()

    def cross_copy(step, layer):
        block = patches.at[first_own + layer]
        return remote(
            block, block, cross_send.at[step - 1, layer], cross_recv.at[step - 1, layer],
            slab=lax.rem(group + step, groups) * 2 + side,
        )

    def origin(step, of_side):
        return (lax.rem(group + groups - step, groups) * 2 + of_side) * layers

    def cross_arrival(step, layer):
        block = patches.at[origin(step, side) + layer]
        return remote(
            block, block, cross_send.at[step - 1, layer], cross_recv.at[step - 1, layer],
            slab=lax.rem(group + step, groups) * 2 + side,
        )

    def pair_copy(step, layer):
        block = patches.at[origin(step, side) + layer]
        return remote(
            block, block, pair_send.at[step, layer], pair_recv.at[step, layer], slab=partner
        )

    def pair_arrival(step, layer):
        block = patches.at[origin(step, 1 - side) + layer]
        return remote(
            block, block, pair_send.at[step, layer], pair_recv.at[step, layer], slab=partner
        )

    def take_rows(layer):
        tile_copy(layer).wait_recv()
        for p in range(count):
            both = jnp.concatenate([cut_own[layer, p], low[layer, p]], axis=0)
            pick = one_hot((window, 2 * window), 1, own_rows[p])
            patches[first_own + layer, p] = jnp.dot(
                pick, both, preferred_element_type=F32
            ).astype(BF16)
        pair_copy(0, layer).start()
        for step in range(1, groups):
            cross_copy(step, layer).start()

    take_rows(0)

    @pl.when(group > 0)
    def _():
        for layer in range(1, layers):
            take_rows(layer)

    def arrive(j):
        owner, layer = j // layers, lax.rem(j, layers)
        of_group, of_side = owner // 2, lax.rem(owner, 2)
        step = lax.rem(group - of_group + groups, groups)

        @pl.when((of_side == side) & (of_group != group))
        def _():
            cross_arrival(step, layer).wait_recv()
            pair_copy(step, layer).start()

        @pl.when(of_side != side)
        def _():
            pair_arrival(step, layer).wait_recv()

    table.wait()
    run = functools.partial(transform, right=right, window=window)
    start = (probe[0].astype(F32), probe[1].astype(F32))
    store(psi, 0, [start] * count)

    def propagator():
        return halves(work[count], window)

    def forward(j, carried):
        @pl.when((group == 0) & (j >= 1) & (j < layers))
        def _():
            take_rows(j)

        arrive(j)
        chi = [
            times(a, b)
            for a, b in zip(load(psi, j, count, window), load(patches, j, count, window))
        ]
        moved = run(chi)
        prop = propagator()
        back = run([conj(times(prop, f)) for f in moved])
        store(psi, j + 1, [conj(f) for f in back])
        return carried

    lax.fori_loop(0, last, forward, 0)
    arrive(last)
    chi = [
        times(a, b)
        for a, b in zip(load(psi, last, count, window), load(patches, last, count, window))
    ]
    far = run(chi)
    shaped = []
    for p, (re, im) in enumerate(far):
        misfit = re * re + im * im - turned[p]
        shaped.append((misfit * re, -(misfit * im)))
    grad = [conj(f) for f in run(shaped)]
    for p in range(count):
        work[p] = jnp.concatenate(grad[p], axis=1)

    def spill_copy(layer):
        return remote(
            spill.at[layer], spilled.at[layer], back_send.at[layer], back_recv.at[layer], tile=after
        )

    def own_term(j):
        @pl.when((j >= first_own) & (j < first_own + layers))
        def _():
            layer = j - first_own
            for p in range(count):
                term = jnp.concatenate(
                    conj_times(halves(psi[j, p], window), halves(work[p], window)), axis=1
                )
                pick = one_hot((2 * window, window), 0, own_rows[p])
                placed = jnp.dot(
                    jnp.concatenate([pick, pick], axis=1),
                    jnp.concatenate(split(term), axis=0),
                    preferred_element_type=F32,
                )
                terms[layer, p] = placed[:window]
                spill[layer, p] = placed[window:].astype(BF16)
            spill_copy(layer).start()

    def backward(i, carried):
        j = last - i
        own_term(j)
        grads = [halves(work[p], window) for p in range(count)]
        inner = [conj_times(a, b) for a, b in zip(load(patches, j, count, window), grads)]
        moved = run(inner)
        prop = propagator()
        back = run([conj(conj_times(prop, f)) for f in moved])
        for p in range(count):
            work[p] = jnp.concatenate(conj(back[p]), axis=1)
        return carried

    lax.fori_loop(0, last - first_own, backward, 0)
    own_term(first_own)

    own_place = jnp.concatenate([one_hot((window, columns), 1, c) for c in own_cols], axis=0)
    prior_place = jnp.concatenate([one_hot((window, columns), 1, c) for c in prior_cols], axis=0)

    def by_part(ref, layer):
        wide = [halves(ref[layer, p], window) for p in range(count)]
        return jnp.concatenate(
            [jnp.concatenate([w[part] for w in wide], axis=1) for part in range(2)], axis=0
        )

    for layer in reversed(range(layers)):
        high, low_part = split(by_part(terms, layer))
        total = jnp.dot(high, own_place, preferred_element_type=F32)
        total += jnp.dot(low_part, own_place, preferred_element_type=F32)
        spill_copy(layer).wait_recv()
        total += jnp.dot(by_part(spilled, layer), prior_place, preferred_element_type=F32)
        out[0, layer] = total[:window].astype(out.dtype)
        out[1, layer] = total[window:].astype(out.dtype)

    @pl.when(side == 1)
    def _():
        for layer in range(layers):
            tile_copy(layer).wait_send()

    for layer in range(layers):
        spill_copy(layer).wait_send()
        for step in range(1, groups):
            cross_copy(step, layer).wait_send()
        for step in range(groups):
            pair_copy(step, layer).wait_send()


def body(object_field, probe_wave, prop_phase, intensity, patch_rows, patch_cols):
    window = probe_wave.shape[1]
    layers = object_field.shape[1]
    count = intensity.shape[0]
    tiles, sections = lax.axis_size("tile"), lax.axis_size("slab")
    slices = sections * layers
    groups = sections // 2
    right = fourier_parts(window)
    wide = (layers, count, window, 2 * window)
    dma = pltpu.SemaphoreType.DMA
    return pl.pallas_call(
        functools.partial(kernel, tiles, sections),
        out_shape=jax.ShapeDtypeStruct(object_field.shape, F32),
        in_specs=[pl.BlockSpec(memory_space=pltpu.SMEM)] * 2
        + [pl.BlockSpec(memory_space=pltpu.VMEM)] * 4
        + [pl.BlockSpec(memory_space=pl.ANY)],
        out_specs=pl.BlockSpec(memory_space=pltpu.VMEM),
        scratch_shapes=[
            pltpu.VMEM(wide, BF16),
            pltpu.VMEM(wide, BF16),
            pltpu.VMEM(wide, BF16),
            pltpu.VMEM((slices,) + wide[1:], BF16),
            pltpu.VMEM((slices,) + wide[1:], F32),
            pltpu.VMEM((count + 1, window, 2 * window), F32),
            pltpu.VMEM(wide, F32),
            pltpu.VMEM(wide, BF16),
            pltpu.VMEM(wide, BF16),
            pltpu.VMEM(right.shape, BF16),
            pltpu.VMEM(intensity.shape, F32),
            dma((layers,)),
            dma((layers,)),
            dma((groups - 1, layers)),
            dma((groups - 1, layers)),
            dma((groups, layers)),
            dma((groups, layers)),
            dma((layers,)),
            dma((layers,)),
            dma(()),
            pltpu.SemaphoreType.REGULAR,
        ],
        compiler_params=pltpu.CompilerParams(
            collective_id=0, has_side_effects=True, vmem_limit_bytes=60 * 1024 * 1024
        ),
    )(
        patch_rows, patch_cols, object_field, probe_wave, prop_phase, intensity,
        jnp.asarray(right),
    ).astype(BF16)


def solution(mesh):
    return jax.shard_map(
        body,
        mesh=mesh,
        in_specs=(P(None, "slab", "tile", None), P(), P(), P("tile", None, None), P(), P()),
        out_specs=P(None, "slab", "tile", None),
        check_vma=False,
    )
```

```python
import functools
import math

import jax
import jax.numpy as jnp
import numpy as np
from jax import lax
from jax.experimental import pallas as pl
from jax.experimental.pallas import tpu as pltpu
from jax.sharding import PartitionSpec as P

F32 = jnp.float32
BF16 = jnp.bfloat16


def fourier_parts(window):
    index = np.arange(window)
    angle = (index[:, None] * index[None, :] % window) * (-2.0 * math.pi / window)
    real = np.cos(angle) / math.sqrt(window)
    imag = np.sin(angle) / math.sqrt(window)
    big = np.block([[real, imag], [-imag, real]]).astype(np.float32)
    high = big.astype(BF16)
    low = (big - high.astype(np.float32)).astype(BF16)
    return np.concatenate([high, high, low], axis=0)


def split(value):
    high = value.astype(BF16)
    return high, (value - high.astype(F32)).astype(BF16)


def from_right(field, right, window):
    high, low = split(jnp.concatenate(field, axis=1))
    product = jnp.dot(
        jnp.concatenate([high, low, high], axis=1), right[...], preferred_element_type=F32
    )
    return product[:, :window], product[:, window:]


def transform(field, right, window):
    first = [from_right(f, right, window) for f in field]
    return [from_right((re.T, im.T), right, window) for re, im in first]


def times(a, b):
    return a[0] * b[0] - a[1] * b[1], a[0] * b[1] + a[1] * b[0]


def conj_times(a, b):
    return a[0] * b[0] + a[1] * b[1], a[0] * b[1] - a[1] * b[0]


def conj(a):
    return a[0], -a[1]


def load(ref, lead, count, window):
    out = []
    for p in range(count):
        block = ref[lead, p].astype(F32)
        out.append((block[:, :window], block[:, window:]))
    return out


def store(ref, lead, field):
    for p, (re, im) in enumerate(field):
        ref[lead, p] = jnp.concatenate([re, im], axis=1).astype(ref.dtype)


MESH = pl.DeviceIdType.MESH


def one_hot(shape, along, offset):
    here = lax.broadcasted_iota(jnp.int32, shape, along)
    there = lax.broadcasted_iota(jnp.int32, shape, 1 - along)
    return jnp.where(here == there + offset, 1.0, 0.0).astype(BF16)


def halves(block, window):
    return block[:, :window], block[:, window:]


def kernel(
    tiles, sections, row_ref, col_ref, obj, probe, phase, measured, right_in, out,
    cut_prior, cut_own, low, patches, psi, work, terms, spill, spilled, right, turned,
    tile_send, tile_recv, cross_send, cross_recv, pair_send, pair_recv, back_send, back_recv, table_sem, go,
):
    layers, window, columns = obj.shape[1], obj.shape[2], obj.shape[3]
    count, slices = measured.shape[0], patches.shape[0]
    groups = sections // 2
    last = slices - 1
    tile = lax.axis_index("tile")
    slab = lax.axis_index("slab")
    after, prior = lax.rem(tile + 1, tiles), lax.rem(tile + tiles - 1, tiles)
    group, side = slab // 2, lax.rem(slab, 2)
    partner = slab + 1 - 2 * side
    first_own = slab * layers

    def remote(src, dst, send, recv, **device):
        return pltpu.make_async_remote_copy(
            src_ref=src, dst_ref=dst, send_sem=send, recv_sem=recv,
            device_id=device, device_id_type=MESH,
        )

    table = pltpu.make_async_copy(right_in, right, table_sem)
    table.start()
    barrier = pltpu.get_barrier_semaphore()
    greeted = [{"tile": after}, {"tile": prior}, {"slab": partner}]
    for step in range(1, groups):
        greeted.append({"slab": lax.rem(group + step, groups) * 2 + side})
    for device in greeted:
        pl.semaphore_signal(barrier, inc=1, device_id=device, device_id_type=MESH)

    def columns_of(base):
        return [col_ref[base * count + p] for p in range(count)]

    prior_cols, own_cols = columns_of(prior), columns_of(tile)
    own_rows = [row_ref[tile * count + p] for p in range(count)]

    def cut(cols, layer, target):
        pick = jnp.concatenate([one_hot((columns, window), 0, c) for c in cols], axis=1)
        both = jnp.concatenate([obj[0, layer], obj[1, layer]], axis=0)
        got = jnp.dot(both, pick, preferred_element_type=F32).astype(BF16)
        for p in range(count):
            part = got[:, p * window : (p + 1) * window]
            target[layer, p] = jnp.concatenate([part[:window], part[window:]], axis=1)

    def tile_copy(layer):
        return remote(
            cut_prior.at[layer], low.at[layer], tile_send.at[layer], tile_recv.at[layer], tile=prior
        )

    for layer in range(layers):
        cut(prior_cols, layer, cut_prior)
    pl.semaphore_wait(barrier, len(greeted))

    @pl.when(side == 0)
    def _():
        for layer in range(layers):
            tile_copy(layer).start()

    for layer in range(layers):
        cut(own_cols, layer, cut_own)
    phase_turned = phase[...].T
    work[count] = jnp.concatenate([jnp.cos(phase_turned), jnp.sin(phase_turned)], axis=1)
    for p in range(count):
        turned[p] = measured[p].T

    @pl.when(side == 0)
    def _():
        for layer in range(layers):
            tile_copy(layer).wait_send()
        pl.semaphore_signal(go, inc=1, device_id={"slab": partner}, device_id_type=MESH)

    @pl.when(side == 1)
    def _():
        pl.semaphore_wait(go, 1)
        for layer in range(layers):
            tile_copy(layer).start()

    def cross_copy(step, layer):
        block = patches.at[first_own + layer]
        return remote(
            block, block, cross_send.at[step - 1, layer], cross_recv.at[step - 1, layer],
            slab=lax.rem(group + step, groups) * 2 + side,
        )

    def origin(step, of_side):
        return (lax.rem(group + groups - step, groups) * 2 + of_side) * layers

    def cross_arrival(step, layer):
        block = patches.at[origin(step, side) + layer]
        return remote(
            block, block, cross_send.at[step - 1, layer], cross_recv.at[step - 1, layer],
            slab=lax.rem(group + step, groups) * 2 + side,
        )

    def pair_copy(step, layer):
        block = patches.at[origin(step, side) + layer]
        return remote(
            block, block, pair_send.at[step, layer], pair_recv.at[step, layer], slab=partner
        )

    def pair_arrival(step, layer):
        block = patches.at[origin(step, 1 - side) + layer]
        return remote(
            block, block, pair_send.at[step, layer], pair_recv.at[step, layer], slab=partner
        )

    def take_rows(layer):
        tile_copy(layer).wait_recv()
        for p in range(count):
            both = jnp.concatenate([cut_own[layer, p], low[layer, p]], axis=0)
            pick = one_hot((window, 2 * window), 1, own_rows[p])
            patches[first_own + layer, p] = jnp.dot(
                pick, both, preferred_element_type=F32
            ).astype(BF16)
        pair_copy(0, layer).start()
        for step in range(1, groups):
            cross_copy(step, layer).start()

    take_rows(0)

    @pl.when(group > 0)
    def _():
        for layer in range(1, layers):
            take_rows(layer)

    def arrive(j):
        owner, layer = j // layers, lax.rem(j, layers)
        of_group, of_side = owner // 2, lax.rem(owner, 2)
        step = lax.rem(group - of_group + groups, groups)

        @pl.when((of_side == side) & (of_group != group))
        def _():
            cross_arrival(step, layer).wait_recv()
            pair_copy(step, layer).start()

        @pl.when(of_side != side)
        def _():
            pair_arrival(step, layer).wait_recv()

    table.wait()
    run = functools.partial(transform, right=right, window=window)
    start = (probe[0].astype(F32), probe[1].astype(F32))
    store(psi, 0, [start] * count)

    def propagator():
        return halves(work[count], window)

    def forward(j, carried):
        @pl.when((group == 0) & (j >= 1) & (j < layers))
        def _():
            take_rows(j)

        arrive(j)
        chi = [
            times(a, b)
            for a, b in zip(load(psi, j, count, window), load(patches, j, count, window))
        ]
        moved = run(chi)
        prop = propagator()
        back = run([conj(times(prop, f)) for f in moved])
        store(psi, j + 1, [conj(f) for f in back])
        return carried

    lax.fori_loop(0, last, forward, 0)
    arrive(last)
    chi = [
        times(a, b)
        for a, b in zip(load(psi, last, count, window), load(patches, last, count, window))
    ]
    far = run(chi)
    shaped = []
    for p, (re, im) in enumerate(far):
        misfit = re * re + im * im - turned[p]
        shaped.append((misfit * re, -(misfit * im)))
    grad = [conj(f) for f in run(shaped)]
    for p in range(count):
        work[p] = jnp.concatenate(grad[p], axis=1)

    def spill_copy(layer, p):
        return remote(
            spill.at[layer, p], spilled.at[layer, p],
            back_send.at[layer, p], back_recv.at[layer, p], tile=after,
        )

    def own_term(j):
        @pl.when((j >= first_own) & (j < first_own + layers))
        def _():
            layer = j - first_own
            for p in range(count):
                term = jnp.concatenate(
                    conj_times(halves(psi[j, p], window), halves(work[p], window)), axis=1
                )
                pick = one_hot((2 * window, window), 0, own_rows[p])
                placed = jnp.dot(
                    jnp.concatenate([pick, pick], axis=1),
                    jnp.concatenate(split(term), axis=0),
                    preferred_element_type=F32,
                )
                terms[layer, p] = placed[:window]
                spill[layer, p] = placed[window:].astype(BF16)
                spill_copy(layer, p).start()

    def backward(i, carried):
        j = last - i
        own_term(j)
        grads = [halves(work[p], window) for p in range(count)]
        inner = [conj_times(a, b) for a, b in zip(load(patches, j, count, window), grads)]
        moved = run(inner)
        prop = propagator()
        back = run([conj(conj_times(prop, f)) for f in moved])
        for p in range(count):
            work[p] = jnp.concatenate(conj(back[p]), axis=1)
        return carried

    lax.fori_loop(0, last - first_own, backward, 0)
    own_term(first_own)

    own_place = jnp.concatenate([one_hot((window, columns), 1, c) for c in own_cols], axis=0)
    prior_place = jnp.concatenate([one_hot((window, columns), 1, c) for c in prior_cols], axis=0)

    def by_part(ref, layer):
        wide = [halves(ref[layer, p], window) for p in range(count)]
        return jnp.concatenate(
            [jnp.concatenate([w[part] for w in wide], axis=1) for part in range(2)], axis=0
        )

    for layer in reversed(range(layers)):
        high, low_part = split(by_part(terms, layer))
        total = jnp.dot(high, own_place, preferred_element_type=F32)
        total += jnp.dot(low_part, own_place, preferred_element_type=F32)
        for p in range(count):
            spill_copy(layer, p).wait_recv()
        total += jnp.dot(by_part(spilled, layer), prior_place, preferred_element_type=F32)
        out[0, layer] = total[:window].astype(out.dtype)
        out[1, layer] = total[window:].astype(out.dtype)

    @pl.when(side == 1)
    def _():
        for layer in range(layers):
            tile_copy(layer).wait_send()

    for layer in range(layers):
        for p in range(count):
            spill_copy(layer, p).wait_send()
        for step in range(1, groups):
            cross_copy(step, layer).wait_send()
        for step in range(groups):
            pair_copy(step, layer).wait_send()


def body(object_field, probe_wave, prop_phase, intensity, patch_rows, patch_cols):
    window = probe_wave.shape[1]
    layers = object_field.shape[1]
    count = intensity.shape[0]
    tiles, sections = lax.axis_size("tile"), lax.axis_size("slab")
    slices = sections * layers
    groups = sections // 2
    right = fourier_parts(window)
    wide = (layers, count, window, 2 * window)
    dma = pltpu.SemaphoreType.DMA
    return pl.pallas_call(
        functools.partial(kernel, tiles, sections),
        out_shape=jax.ShapeDtypeStruct(object_field.shape, BF16),
        in_specs=[pl.BlockSpec(memory_space=pltpu.SMEM)] * 2
        + [pl.BlockSpec(memory_space=pltpu.VMEM)] * 4
        + [pl.BlockSpec(memory_space=pl.ANY)],
        out_specs=pl.BlockSpec(memory_space=pltpu.VMEM),
        scratch_shapes=[
            pltpu.VMEM(wide, BF16),
            pltpu.VMEM(wide, BF16),
            pltpu.VMEM(wide, BF16),
            pltpu.VMEM((slices,) + wide[1:], BF16),
            pltpu.VMEM((slices,) + wide[1:], F32),
            pltpu.VMEM((count + 1, window, 2 * window), F32),
            pltpu.VMEM(wide, F32),
            pltpu.VMEM(wide, BF16),
            pltpu.VMEM(wide, BF16),
            pltpu.VMEM(right.shape, BF16),
            pltpu.VMEM(intensity.shape, F32),
            dma((layers,)),
            dma((layers,)),
            dma((groups - 1, layers)),
            dma((groups - 1, layers)),
            dma((groups, layers)),
            dma((groups, layers)),
            dma((layers, count)),
            dma((layers, count)),
            dma(()),
            pltpu.SemaphoreType.REGULAR,
        ],
        compiler_params=pltpu.CompilerParams(
            collective_id=0, has_side_effects=True, vmem_limit_bytes=60 * 1024 * 1024
        ),
    )(
        patch_rows, patch_cols, object_field, probe_wave, prop_phase, intensity,
        jnp.asarray(right),
    )


def solution(mesh):
    return jax.shard_map(
        body,
        mesh=mesh,
        in_specs=(P(None, "slab", "tile", None), P(), P(), P("tile", None, None), P(), P()),
        out_specs=P(None, "slab", "tile", None),
        check_vma=False,
    )
```

```python
import functools
import math

import jax
import jax.numpy as jnp
import numpy as np
from jax import lax
from jax.experimental import pallas as pl
from jax.experimental.pallas import tpu as pltpu
from jax.sharding import PartitionSpec as P

F32 = jnp.float32
BF16 = jnp.bfloat16


def fourier_parts(window):
    index = np.arange(window)
    angle = (index[:, None] * index[None, :] % window) * (-2.0 * math.pi / window)
    real = np.cos(angle) / math.sqrt(window)
    imag = np.sin(angle) / math.sqrt(window)
    big = np.block([[real, imag], [-imag, real]]).astype(np.float32)
    high = big.astype(BF16)
    low = (big - high.astype(np.float32)).astype(BF16)
    return np.concatenate([high, high, low], axis=0)


def split(value):
    high = value.astype(BF16)
    return high, (value - high.astype(F32)).astype(BF16)


def from_right(field, right, window):
    high, low = split(jnp.concatenate(field, axis=1))
    product = jnp.dot(
        jnp.concatenate([high, low, high], axis=1), right[...], preferred_element_type=F32
    )
    return product[:, :window], product[:, window:]


def transform(field, right, window):
    first = [from_right(f, right, window) for f in field]
    return [from_right((re.T, im.T), right, window) for re, im in first]


def times(a, b):
    return a[0] * b[0] - a[1] * b[1], a[0] * b[1] + a[1] * b[0]


def conj_times(a, b):
    return a[0] * b[0] + a[1] * b[1], a[0] * b[1] - a[1] * b[0]


def conj(a):
    return a[0], -a[1]


def load(ref, lead, count, window):
    out = []
    for p in range(count):
        block = ref[lead, p].astype(F32)
        out.append((block[:, :window], block[:, window:]))
    return out


def store(ref, lead, field):
    for p, (re, im) in enumerate(field):
        ref[lead, p] = jnp.concatenate([re, im], axis=1).astype(ref.dtype)


MESH = pl.DeviceIdType.MESH


def one_hot(shape, along, offset):
    here = lax.broadcasted_iota(jnp.int32, shape, along)
    there = lax.broadcasted_iota(jnp.int32, shape, 1 - along)
    return jnp.where(here == there + offset, 1.0, 0.0).astype(BF16)


def halves(block, window):
    return block[:, :window], block[:, window:]


def kernel(
    tiles, sections, row_ref, col_ref, obj, probe, phase, measured, right_in, out,
    cut_prior, cut_own, low, patches, psi, work, terms, spill, spilled, right, turned,
    tile_send, tile_recv, cross_send, cross_recv, pair_send, pair_recv, back_send, back_recv, table_sem, go,
):
    layers, window, columns = obj.shape[1], obj.shape[2], obj.shape[3]
    count, slices = measured.shape[0], patches.shape[0]
    groups = sections // 2
    last = slices - 1
    tile = lax.axis_index("tile")
    slab = lax.axis_index("slab")
    after, prior = lax.rem(tile + 1, tiles), lax.rem(tile + tiles - 1, tiles)
    group, side = slab // 2, lax.rem(slab, 2)
    partner = slab + 1 - 2 * side
    first_own = slab * layers

    def remote(src, dst, send, recv, **device):
        return pltpu.make_async_remote_copy(
            src_ref=src, dst_ref=dst, send_sem=send, recv_sem=recv,
            device_id=device, device_id_type=MESH,
        )

    table = pltpu.make_async_copy(right_in, right, table_sem)
    table.start()
    barrier = pltpu.get_barrier_semaphore()
    greeted = [{"tile": after}, {"tile": prior}, {"slab": partner}]
    for step in range(1, groups):
        greeted.append({"slab": lax.rem(group + step, groups) * 2 + side})
    for device in greeted:
        pl.semaphore_signal(barrier, inc=1, device_id=device, device_id_type=MESH)

    def columns_of(base):
        return [col_ref[base * count + p] for p in range(count)]

    prior_cols, own_cols = columns_of(prior), columns_of(tile)
    own_rows = [row_ref[tile * count + p] for p in range(count)]

    def cut(cols, layer, target):
        pick = jnp.concatenate([one_hot((columns, window), 0, c) for c in cols], axis=1)
        both = jnp.concatenate([obj[0, layer], obj[1, layer]], axis=0)
        got = jnp.dot(both, pick, preferred_element_type=F32).astype(BF16)
        for p in range(count):
            part = got[:, p * window : (p + 1) * window]
            target[layer, p] = jnp.concatenate([part[:window], part[window:]], axis=1)

    def tile_copy(layer):
        return remote(
            cut_prior.at[layer], low.at[layer], tile_send.at[layer], tile_recv.at[layer], tile=prior
        )

    for layer in range(layers):
        cut(prior_cols, layer, cut_prior)
    pl.semaphore_wait(barrier, len(greeted))

    @pl.when(side == 0)
    def _():
        for layer in range(layers):
            tile_copy(layer).start()

    for layer in range(layers):
        cut(own_cols, layer, cut_own)
    phase_turned = phase[...].T
    work[count] = jnp.concatenate([jnp.cos(phase_turned), jnp.sin(phase_turned)], axis=1)
    for p in range(count):
        turned[p] = measured[p].T

    @pl.when(side == 0)
    def _():
        for layer in range(layers):
            tile_copy(layer).wait_send()
        pl.semaphore_signal(go, inc=1, device_id={"slab": partner}, device_id_type=MESH)

    @pl.when(side == 1)
    def _():
        pl.semaphore_wait(go, 1)
        for layer in range(layers):
            tile_copy(layer).start()

    def cross_copy(step, layer):
        block = patches.at[first_own + layer]
        return remote(
            block, block, cross_send.at[step - 1, layer], cross_recv.at[step - 1, layer],
            slab=lax.rem(group + step, groups) * 2 + side,
        )

    def origin(step, of_side):
        return (lax.rem(group + groups - step, groups) * 2 + of_side) * layers

    def cross_arrival(step, layer):
        block = patches.at[origin(step, side) + layer]
        return remote(
            block, block, cross_send.at[step - 1, layer], cross_recv.at[step - 1, layer],
            slab=lax.rem(group + step, groups) * 2 + side,
        )

    def pair_copy(step, layer):
        block = patches.at[origin(step, side) + layer]
        return remote(
            block, block, pair_send.at[step, layer], pair_recv.at[step, layer], slab=partner
        )

    def pair_arrival(step, layer):
        block = patches.at[origin(step, 1 - side) + layer]
        return remote(
            block, block, pair_send.at[step, layer], pair_recv.at[step, layer], slab=partner
        )

    def take_rows(layer):
        tile_copy(layer).wait_recv()
        for p in range(count):
            both = jnp.concatenate([cut_own[layer, p], low[layer, p]], axis=0)
            pick = one_hot((window, 2 * window), 1, own_rows[p])
            patches[first_own + layer, p] = jnp.dot(
                pick, both, preferred_element_type=F32
            ).astype(BF16)
        pair_copy(0, layer).start()
        for step in range(1, groups):
            cross_copy(step, layer).start()

    take_rows(0)

    @pl.when(group > 0)
    def _():
        for layer in range(1, layers):
            take_rows(layer)

    def arrive(j):
        owner, layer = j // layers, lax.rem(j, layers)
        of_group, of_side = owner // 2, lax.rem(owner, 2)
        step = lax.rem(group - of_group + groups, groups)

        @pl.when((of_side == side) & (of_group != group))
        def _():
            cross_arrival(step, layer).wait_recv()
            pair_copy(step, layer).start()

        @pl.when(of_side != side)
        def _():
            pair_arrival(step, layer).wait_recv()

    table.wait()
    run = functools.partial(transform, right=right, window=window)
    start = (probe[0].astype(F32), probe[1].astype(F32))
    store(psi, 0, [start] * count)

    def propagator():
        return halves(work[count], window)

    def forward(j, carried):
        @pl.when((group == 0) & (j >= 1) & (j < layers))
        def _():
            take_rows(j)

        arrive(j)
        chi = [
            times(a, b)
            for a, b in zip(load(psi, j, count, window), load(patches, j, count, window))
        ]
        moved = run(chi)
        prop = propagator()
        back = run([conj(times(prop, f)) for f in moved])
        store(psi, j + 1, [conj(f) for f in back])
        return carried

    lax.fori_loop(0, last, forward, 0)
    arrive(last)
    chi = [
        times(a, b)
        for a, b in zip(load(psi, last, count, window), load(patches, last, count, window))
    ]
    far = run(chi)
    shaped = []
    for p, (re, im) in enumerate(far):
        misfit = re * re + im * im - turned[p]
        shaped.append((misfit * re, -(misfit * im)))
    grad = [conj(f) for f in run(shaped)]
    for p in range(count):
        work[p] = jnp.concatenate(grad[p], axis=1)

    def spill_copy(layer, p):
        return remote(
            spill.at[layer, p], spilled.at[layer, p],
            back_send.at[layer, p], back_recv.at[layer, p], tile=after,
        )

    def own_term(j):
        @pl.when((j >= first_own) & (j < first_own + layers))
        def _():
            layer = j - first_own
            for p in range(count):
                term = jnp.concatenate(
                    conj_times(halves(psi[j, p], window), halves(work[p], window)), axis=1
                )
                parts = jnp.concatenate(split(term), axis=0)
                pick = one_hot((window, window), 0, own_rows[p] - window)
                spill[layer, p] = jnp.dot(
                    jnp.concatenate([pick, pick], axis=1), parts, preferred_element_type=F32
                ).astype(BF16)
                spill_copy(layer, p).start()
                pick = one_hot((window, window), 0, own_rows[p])
                terms[layer, p] = jnp.dot(
                    jnp.concatenate([pick, pick], axis=1), parts, preferred_element_type=F32
                )

    def backward(i, carried):
        j = last - i
        own_term(j)
        grads = [halves(work[p], window) for p in range(count)]
        inner = [conj_times(a, b) for a, b in zip(load(patches, j, count, window), grads)]
        moved = run(inner)
        prop = propagator()
        back = run([conj(conj_times(prop, f)) for f in moved])
        for p in range(count):
            work[p] = jnp.concatenate(conj(back[p]), axis=1)
        return carried

    lax.fori_loop(0, last - first_own, backward, 0)
    own_term(first_own)

    own_place = jnp.concatenate([one_hot((window, columns), 1, c) for c in own_cols], axis=0)
    prior_place = jnp.concatenate([one_hot((window, columns), 1, c) for c in prior_cols], axis=0)

    def by_part(ref, layer):
        wide = [halves(ref[layer, p], window) for p in range(count)]
        return jnp.concatenate(
            [jnp.concatenate([w[part] for w in wide], axis=1) for part in range(2)], axis=0
        )

    for layer in reversed(range(layers)):
        high, low_part = split(by_part(terms, layer))
        total = jnp.dot(high, own_place, preferred_element_type=F32)
        total += jnp.dot(low_part, own_place, preferred_element_type=F32)
        for p in range(count):
            spill_copy(layer, p).wait_recv()
        total += jnp.dot(by_part(spilled, layer), prior_place, preferred_element_type=F32)
        out[0, layer] = total[:window].astype(out.dtype)
        out[1, layer] = total[window:].astype(out.dtype)

    @pl.when(side == 1)
    def _():
        for layer in range(layers):
            tile_copy(layer).wait_send()

    for layer in range(layers):
        for p in range(count):
            spill_copy(layer, p).wait_send()
        for step in range(1, groups):
            cross_copy(step, layer).wait_send()
        for step in range(groups):
            pair_copy(step, layer).wait_send()


def body(object_field, probe_wave, prop_phase, intensity, patch_rows, patch_cols):
    window = probe_wave.shape[1]
    layers = object_field.shape[1]
    count = intensity.shape[0]
    tiles, sections = lax.axis_size("tile"), lax.axis_size("slab")
    slices = sections * layers
    groups = sections // 2
    right = fourier_parts(window)
    wide = (layers, count, window, 2 * window)
    dma = pltpu.SemaphoreType.DMA
    return pl.pallas_call(
        functools.partial(kernel, tiles, sections),
        out_shape=jax.ShapeDtypeStruct(object_field.shape, BF16),
        in_specs=[pl.BlockSpec(memory_space=pltpu.SMEM)] * 2
        + [pl.BlockSpec(memory_space=pltpu.VMEM)] * 4
        + [pl.BlockSpec(memory_space=pl.ANY)],
        out_specs=pl.BlockSpec(memory_space=pltpu.VMEM),
        scratch_shapes=[
            pltpu.VMEM(wide, BF16),
            pltpu.VMEM(wide, BF16),
            pltpu.VMEM(wide, BF16),
            pltpu.VMEM((slices,) + wide[1:], BF16),
            pltpu.VMEM((slices,) + wide[1:], F32),
            pltpu.VMEM((count + 1, window, 2 * window), F32),
            pltpu.VMEM(wide, F32),
            pltpu.VMEM(wide, BF16),
            pltpu.VMEM(wide, BF16),
            pltpu.VMEM(right.shape, BF16),
            pltpu.VMEM(intensity.shape, F32),
            dma((layers,)),
            dma((layers,)),
            dma((groups - 1, layers)),
            dma((groups - 1, layers)),
            dma((groups, layers)),
            dma((groups, layers)),
            dma((layers, count)),
            dma((layers, count)),
            dma(()),
            pltpu.SemaphoreType.REGULAR,
        ],
        compiler_params=pltpu.CompilerParams(
            collective_id=0, has_side_effects=True, vmem_limit_bytes=60 * 1024 * 1024
        ),
    )(
        patch_rows, patch_cols, object_field, probe_wave, prop_phase, intensity,
        jnp.asarray(right),
    )


def solution(mesh):
    return jax.shard_map(
        body,
        mesh=mesh,
        in_specs=(P(None, "slab", "tile", None), P(), P(), P("tile", None, None), P(), P()),
        out_specs=P(None, "slab", "tile", None),
        check_vma=False,
    )
```
